512 devices in a mesh: dp: 16 (over z), seq: 32 (over x, y, core).
Axes of the slice: x: 4, y: 4, z: 16, core: 2. Of those that a mesh axis runs over, the one named last changes fastest.
Arguments:
- query_rows: bfloat16 [65536, 4096], P(('dp', 'seq')), may hold values from -10 to 10
- source_key_rows: bfloat16 [65536, 1024], P(('dp', 'seq')), may hold values from -10 to 10
- source_value_rows: bfloat16 [65536, 1024], P(('dp', 'seq')), may hold values from -6 to 6
- grad_rows: bfloat16 [65536, 4096], P(('dp', 'seq')), may hold values from -6 to 6
- routes: int32 [65536, 1], P(('dp', 'seq')), may hold values from 0 to 15; in each aligned block of 128 rows (0 to 127, 128 to 255, ...) at most 8 rows name the same one
- segments: int32 [16, 4096], P('dp', 'seq'), may hold values from 0 to 15, never falling along the last dimension, each value on 1 to 512 neighbouring positions
Outputs:
- grad_query: bfloat16 [65536, 4096], P(('dp', 'seq'))
- packed_key_gradient: bfloat16 [65536, 1024], P(('dp', 'seq'))
- packed_value_gradient: bfloat16 [65536, 1024], P(('dp', 'seq'))
The draws below stay inside these ranges and needn't reach their ends.
Inputs may be any that keep to these rules, and one draw needn't show every extreme that they name: `routes`: each pack number is named by exactly 8 of the rows of one device. `segments`: along a pack the document numbers never fall; a document covers 1 to 512 consecutive positions, and some document exactly 512.
All inputs are finite; a program needn't handle non-finite values.
Results may differ from the reference program's by a relative error of at most 0.012.
The reference program's roundings to bfloat16 on the way (of `prob_low` and `grad_score`) count: a program that leaves them out, or rounds other values in their place, can miss the bound.
Values may be sent and summed in bfloat16 or wider, within the bound.
A program may use at most 64 MiB of HBM per device.

```python
import math
import jax
import jax.numpy as jnp
import numpy as np
from jax import lax

QUERY_HEADS = 32
KEY_VALUE_HEADS = 8
HEAD_DIMENSION = 128
TOK_DEV = 128
MAXDOC = 512
PACK_POSITIONS = 4096
TOKEN_COUNT = 65536
DOCS = 16
N_DP = 16
N_SEQ = 32


def draw_query_rows(key, part):
    random_perturbation = jnp.clip(jax.random.normal(jax.random.fold_in(key, 11), (TOKEN_COUNT, QUERY_HEADS * HEAD_DIMENSION), jnp.float32), -6.0, 6.0)
    return random_perturbation.astype(jnp.bfloat16)


def draw_source_key_rows(key, part):
    random_perturbation = jnp.clip(jax.random.normal(jax.random.fold_in(key, 21), (TOKEN_COUNT, KEY_VALUE_HEADS * HEAD_DIMENSION), jnp.float32), -6.0, 6.0)
    return random_perturbation.astype(jnp.bfloat16)


def shard_levels(stream_key, shape, cuts, smallest, top_value):
    loudness = 1.0
    for axis_at, parts in cuts:
        draws = jax.random.uniform(jax.random.fold_in(jax.random.fold_in(stream_key, 6), axis_at), (parts,), jnp.float32, smallest / len(cuts), top_value / len(cuts))
        loudness = loudness * jnp.repeat(jnp.exp(draws), shape[axis_at] // parts).reshape((-1,) + (1,) * (len(shape) - 1 - axis_at))
    return loudness


def split_up(amount, total, limit, skew):
    weights = [(1 << 20) // math.isqrt(standing ** skew) + 1 for standing in range(2, amount + 1)]
    surplus, holding = total - limit - (amount - 1), [1] * (amount - 1)
    while surplus > 0:
        movable = [i for i in range(amount - 1) if holding[i] < limit]
        mass, remaining = sum([weights[i] for i in movable]), surplus
        for i in movable:
            more = min(limit - holding[i], max(1, remaining * weights[i] // mass), surplus)
            holding[i] = holding[i] + more
            surplus = surplus - more
    return np.array([limit] + holding)


def uneven(rng, count, total, reach, slope):
    if count == 2:
        one = jax.random.randint(rng, (), max(1, total - reach), min(reach, total - 1) + 1)
        return jnp.stack([one, total - one])
    sizes = jnp.asarray(split_up(count, total, reach, slope), jnp.int32)
    twos = (count - 1) // 2
    donor, taker = sizes[1:1 + 2 * twos:2], sizes[2:2 + 2 * twos:2]
    margin = jnp.minimum(donor - 1, reach - taker)
    passed = jax.random.randint(jax.random.fold_in(rng, 1), (twos,), 0, 1 << 20) % (margin + 1)
    sizes = sizes.at[1:1 + 2 * twos:2].set(donor - passed).at[2:2 + 2 * twos:2].set(taker + passed)
    return sizes[jax.random.permutation(jax.random.fold_in(rng, 2), count)]


def shared_out(stream_key, own, number, rows, amount, top, bound, lean):
    sequence = jax.random.permutation(stream_key, amount)
    crowded, ordinary = shares(amount, rows * top, bound, lean, True), shares(amount, rows * top, bound, lean, False)
    places = jnp.arange(amount)

    def named(sizes, rotation):
        used = int((sizes > 0).sum())
        fixed = max(1, used // 4)
        shifted = fixed + (places - fixed + rotation * (used - fixed)) % max(1, amount - fixed)
        return jnp.zeros((amount,), jnp.int32).at[sequence[jnp.where(places < fixed, places, shifted)]].set(jnp.asarray(sizes, jnp.int32))

    sizes = jnp.where(number % 4 == 0, named(crowded, number // 4), named(ordinary, number - number // 4 - 1))
    mixed = jax.random.permutation(jax.random.fold_in(own, 3), amount)
    giver, receiver = mixed[0:amount // 2 * 2:2], mixed[1:amount // 2 * 2:2]
    room = jnp.minimum(sizes[giver] - 1, bound - sizes[receiver]) // 2
    room = jnp.where((giver == sequence[0]) | (receiver == sequence[0]) | (sizes[receiver] == 0), 0, jnp.maximum(room, 0))
    shifted = jax.random.randint(jax.random.fold_in(own, 4), (amount // 2,), 0, 1 << 20) % (room + 1)
    sizes = sizes.at[giver].add(-shifted).at[receiver].add(shifted)
    items = jnp.searchsorted(jnp.cumsum(sizes), jnp.arange(rows * top), side="right").astype(jnp.int32)
    table = items.reshape(top, rows).T
    table = table[jax.random.permutation(jax.random.fold_in(own, 1), rows)]
    rotation = jax.random.randint(jax.random.fold_in(own, 2), (rows, 1), 0, top)
    return jnp.take_along_axis(table, (jnp.arange(top)[None, :] + rotation) % top, axis=1)


def shares(amount, total, reach, slope, full):
    weights = [(1 << 20) // math.isqrt(grade ** slope) + 1 for grade in range(1, amount + 1)]
    largest = reach if full else min(reach, max(-(-total // amount), total * weights[0] // sum(weights)))
    least = 1 if total - largest >= amount - 1 else 0
    given, surplus = [largest] + [least] * (amount - 1), total - largest - least * (amount - 1)
    while surplus > 0:
        movable = [i for i in range(1, amount) if given[i] < largest] or [i for i in range(1, amount) if given[i] < reach]
        pool, budget = sum([weights[i] for i in movable]), surplus
        for i in movable:
            extra = min(reach - given[i], max(1, budget * weights[i] // pool), surplus)
            given[i] = given[i] + extra
            surplus = surplus - extra
    return np.array(given)


def centred(key, dims, spread, most, pieces=(), kind=jnp.bfloat16):
    array = jax.random.normal(key, dims, jnp.float32) * spread
    if len(pieces) > 0:
        array = shard_levels(key, dims, pieces, -0.22, 0.18) * array
    return jnp.clip(array, min=-most, max=most).astype(kind)


def setup_inputs(seed: int = 0) -> dict:
    arg_keys = jax.random.split(jax.random.key(seed), 7)
    query_rows = draw_query_rows(jax.random.fold_in(arg_keys[6], 71), 0)
    source_key_rows = draw_source_key_rows(jax.random.fold_in(arg_keys[6], 71), 0)
    source_value_rows = centred(arg_keys[2], (TOKEN_COUNT, KEY_VALUE_HEADS * HEAD_DIMENSION), 1.0, 6.0, ((0, 512),))
    grad_rows = centred(arg_keys[3], (TOKEN_COUNT, QUERY_HEADS * HEAD_DIMENSION), 1.0, 6.0, ((0, 512),))
    routes_keys = jax.random.split(jax.random.fold_in(arg_keys[4], 1), TOKEN_COUNT // TOK_DEV)
    routes_turns = jax.random.permutation(jax.random.fold_in(arg_keys[4], 3), TOKEN_COUNT // TOK_DEV)
    routes = jax.vmap(lambda own, number: shared_out(jax.random.fold_in(arg_keys[4], 2), own, number, TOK_DEV, N_DP, 1, TOK_DEV // N_DP, 0))(routes_keys, routes_turns).reshape((TOKEN_COUNT, 1))
    segments = jax.vmap(lambda own: jnp.searchsorted(jnp.cumsum(uneven(own, DOCS, PACK_POSITIONS, MAXDOC, 2)), jnp.arange(PACK_POSITIONS), side="right"))(jax.random.split(arg_keys[5], N_DP)).reshape((N_DP, PACK_POSITIONS)).astype(jnp.int32)
    return {"query_rows": query_rows, "source_key_rows": source_key_rows, "source_value_rows": source_value_rows, "grad_rows": grad_rows, "routes": routes, "segments": segments}


def attend(query_block, key_band, value_band, grad_block, seg_query, seg_keys, offset):
    score_scale = HEAD_DIMENSION ** -0.5
    query_wide = query_block.astype(jnp.float32)
    key_wide = key_band.astype(jnp.float32)
    value_wide = value_band.astype(jnp.float32)
    grad_wide = grad_block.astype(jnp.float32)
    scores = jnp.einsum("ahd,jhd->haj", query_wide, key_wide) * score_scale
    row_pos = jnp.arange(query_block.shape[0], dtype=jnp.int32)[:, None]
    col_pos = jnp.arange(key_band.shape[0], dtype=jnp.int32)[None, :]
    allowed = (col_pos <= row_pos + offset) & (seg_keys[None, :] == seg_query[:, None])
    scores = jnp.where(allowed[None], scores, -jnp.inf)
    top_score = jnp.max(scores, axis=2, keepdims=True)
    weights = jnp.exp(scores - top_score)
    soft_prob = weights / jnp.sum(weights, axis=2, keepdims=True)
    prob_low = soft_prob.astype(jnp.bfloat16).astype(jnp.float32)
    output = jnp.einsum("haj,jhd->ahd", prob_low, value_wide)
    row_delta = jnp.sum(grad_wide * output, axis=2)
    grad_prob = jnp.einsum("ahd,jhd->haj", grad_wide, value_wide)
    grad_score = (soft_prob * (grad_prob - row_delta.T[:, :, None]) * score_scale).astype(jnp.bfloat16).astype(jnp.float32)
    grad_query = jnp.einsum("haj,jhd->ahd", grad_score, key_wide).astype(jnp.bfloat16)
    packed_key_gradient = jnp.einsum("haj,ahd->jhd", grad_score, query_wide)
    packed_value_gradient = jnp.einsum("haj,ahd->jhd", prob_low, grad_wide)
    return grad_query, packed_key_gradient, packed_value_gradient


def group_pass(packed):
    pack_q, packed_key, packed_value, pack_g, seg_all = packed
    group_member_count = QUERY_HEADS // KEY_VALUE_HEADS
    broadened_key = jnp.broadcast_to(packed_key[:, :, None, :], (PACK_POSITIONS, KEY_VALUE_HEADS, group_member_count, HEAD_DIMENSION)).reshape(PACK_POSITIONS, QUERY_HEADS, HEAD_DIMENSION)
    broadened_value = jnp.broadcast_to(packed_value[:, :, None, :], (PACK_POSITIONS, KEY_VALUE_HEADS, group_member_count, HEAD_DIMENSION)).reshape(PACK_POSITIONS, QUERY_HEADS, HEAD_DIMENSION)
    blocks = PACK_POSITIONS // MAXDOC
    query_blocks = pack_q.reshape(blocks, MAXDOC, QUERY_HEADS, HEAD_DIMENSION)
    key_blocks = broadened_key.reshape(blocks, MAXDOC, QUERY_HEADS, HEAD_DIMENSION)
    value_blocks = broadened_value.reshape(blocks, MAXDOC, QUERY_HEADS, HEAD_DIMENSION)
    grad_blocks = pack_g.reshape(blocks, MAXDOC, QUERY_HEADS, HEAD_DIMENSION)
    key_prior = jnp.concatenate([jnp.zeros_like(key_blocks[:1]), key_blocks[:-1]], axis=0)
    value_prior = jnp.concatenate([jnp.zeros_like(value_blocks[:1]), value_blocks[:-1]], axis=0)
    seg_blocks = seg_all.reshape(blocks, MAXDOC).astype(jnp.int32)
    seg_prior = jnp.concatenate([jnp.full((1, MAXDOC), -1, jnp.int32), seg_blocks[:-1]], axis=0)

    def block_step(scan_carry, inputs):
        query_block, key_before, key_own, value_before, value_own, grad_block, seg_before, seg_own = inputs
        result = attend(query_block, jnp.concatenate([key_before, key_own], 0), jnp.concatenate([value_before, value_own], 0), grad_block, seg_own, jnp.concatenate([seg_before, seg_own], 0), MAXDOC)
        return scan_carry, result

    unused, (grad_q, band_k, band_v) = lax.scan(block_step, jnp.int32(0), (query_blocks, key_prior, key_blocks, value_prior, value_blocks, grad_blocks, seg_prior, seg_blocks))

    def fold_band(band_sum):
        own_part = band_sum[:, MAXDOC:]
        later_part = jnp.concatenate([band_sum[1:, :MAXDOC], jnp.zeros_like(band_sum[:1, :MAXDOC])], axis=0)
        return (own_part + later_part).astype(jnp.bfloat16).reshape(PACK_POSITIONS, QUERY_HEADS, HEAD_DIMENSION)

    return grad_q.reshape(PACK_POSITIONS, QUERY_HEADS, HEAD_DIMENSION), fold_band(band_k), fold_band(band_v)


def reference(query_rows, source_key_rows, source_value_rows, grad_rows, routes, segments):
    group_member_count = QUERY_HEADS // KEY_VALUE_HEADS
    capacity = TOK_DEV // N_DP
    index = jnp.arange(TOKEN_COUNT, dtype=jnp.int32)
    home = index // TOK_DEV
    source_group = home // N_SEQ
    source_shard = home % N_SEQ
    targets = routes[:, 0].astype(jnp.int32)
    onehot = (targets[:, None] == jnp.arange(N_DP, dtype=jnp.int32)[None, :]).astype(jnp.int32)
    running = jnp.cumsum(onehot.reshape(N_DP * N_SEQ, TOK_DEV, N_DP), axis=1).reshape(TOKEN_COUNT, N_DP).astype(jnp.int32)
    ranks = jnp.sum((running - onehot) * onehot, axis=1).astype(jnp.int32)
    place = (targets * PACK_POSITIONS + source_shard * TOK_DEV + source_group * capacity + ranks).astype(jnp.int32)

    def relocated(matrix):
        return jnp.zeros_like(matrix).at[place].set(matrix)

    dest_q = relocated(query_rows).reshape(N_DP, PACK_POSITIONS, QUERY_HEADS, HEAD_DIMENSION)
    destination_key = relocated(source_key_rows).reshape(N_DP, PACK_POSITIONS, KEY_VALUE_HEADS, HEAD_DIMENSION)
    destination_value = relocated(source_value_rows).reshape(N_DP, PACK_POSITIONS, KEY_VALUE_HEADS, HEAD_DIMENSION)
    grad_heads = grad_rows.reshape(N_DP, PACK_POSITIONS, QUERY_HEADS, HEAD_DIMENSION)
    grad_q, key_contribution, value_contribution = lax.map(group_pass, (dest_q, destination_key, destination_value, grad_heads, segments))
    grad_query = grad_q.reshape(TOKEN_COUNT, QUERY_HEADS * HEAD_DIMENSION)
    packed_key_gradient = jnp.sum(key_contribution.reshape(TOKEN_COUNT, KEY_VALUE_HEADS, group_member_count, HEAD_DIMENSION).astype(jnp.float32), axis=2).astype(jnp.bfloat16).reshape(TOKEN_COUNT, KEY_VALUE_HEADS * HEAD_DIMENSION)
    packed_value_gradient = jnp.sum(value_contribution.reshape(TOKEN_COUNT, KEY_VALUE_HEADS, group_member_count, HEAD_DIMENSION).astype(jnp.float32), axis=2).astype(jnp.bfloat16).reshape(TOKEN_COUNT, KEY_VALUE_HEADS * HEAD_DIMENSION)
    return (grad_query, packed_key_gradient, packed_value_gradient)
```

```python
import functools

import jax
import jax.numpy as jnp
from jax import lax
from jax.experimental import pallas as pl
from jax.experimental.pallas import tpu as pltpu
from jax.sharding import PartitionSpec as P

MESH = pl.DeviceIdType.MESH
D = 128
GROUP = 4
CHUNKS = 4
NZ = 16
NC = 16
CAP = 8
ROWS = 2 * D
BAND = 5 * D
WIDE = GROUP * D
SCALE = D ** (-0.5)
LOG2E = 1.4426950408889634
NEG = -1e30
F32, BF16 = jnp.float32, jnp.bfloat16


def dot(a, b, ca, cb):
    return lax.dot_general(a, b, (((ca,), (cb,)), ((), ())), preferred_element_type=F32)


def kernel(
    q_ref, k_ref, v_ref, g_ref, routes_ref, seg_ref,
    dq_out, dk_out, dv_out,
    kv_send, kv_recv, q_send, q_recv, g_buf, band, seg_src, seg_band, bias,
    acc_k, acc_v, own, part_send, part_recv, dq_stage, dq_recv, dkv_send, dkv_recv,
    kv_ss, kv_rs, q_ss, q_rs, g_ss, g_rs, seg_ss, seg_rs, halo_ss, halo_rs,
    part_ss, part_rs, dq_ss, dq_rs, dkv_ss, dkv_rs,
):
    z = lax.axis_index("dp")
    s = lax.axis_index("seq")
    c, core = s // 2, s % 2
    other = 1 - core

    def at(dz, dc, to_core):
        return {"dp": (z + dz + NZ) % NZ, "seq": ((c + dc + NC) % NC) * 2 + to_core}

    def remote(src, dst, ssem, rsem, device):
        return pltpu.make_async_remote_copy(
            src_ref=src, dst_ref=dst, send_sem=ssem, recv_sem=rsem,
            device_id=device, device_id_type=MESH,
        )

    def drain(ref, sem):
        pltpu.make_async_copy(ref, ref, sem).wait()

    def step_of(i):
        return (i // 2 + 1) * (1 - 2 * (i % 2))

    barrier = pltpu.get_barrier_semaphore()

    def greet(dz, dc, to_core):
        pl.semaphore_signal(barrier, inc=1, device_id=at(dz, dc, to_core), device_id_type=MESH)

    def greet_z(i, carry):
        greet(step_of(i), 0, core)
        greet(step_of(i), 0, other)
        return carry

    lax.fori_loop(0, NZ - 1, greet_z, 0)
    greet(0, 0, other)
    for dc in (1, 2, -1, -2):
        greet(0, dc, core)
        greet(0, dc, other)

    lane = lax.broadcasted_iota(jnp.int32, (D, D), 1)
    sub = lax.broadcasted_iota(jnp.int32, (D, D), 0)
    routes = routes_ref[...]
    onehot = (routes == lane).astype(F32)
    before = dot((lane < sub).astype(BF16), onehot.astype(BF16), 1, 0)
    rank = jnp.sum(before * onehot, axis=1, keepdims=True)
    slot = routes.astype(F32) * float(CAP) + rank
    order = (slot == lane.astype(F32)).astype(F32).T.astype(BF16)

    def permuted(ref, start):
        moved = dot(order, ref[:, start : start + WIDE], 1, 0)
        return moved.reshape(NZ, CAP, WIDE).astype(BF16)

    for h in range(2):
        kv_send[h * NZ : (h + 1) * NZ, :, :WIDE] = permuted(k_ref, h * WIDE)
        kv_send[h * NZ : (h + 1) * NZ, :, WIDE:] = permuted(v_ref, h * WIDE)
    seg_src[...] = jnp.broadcast_to(seg_ref[...], seg_src.shape)

    pl.semaphore_wait(barrier, 2 * (NZ - 1) + 1 + 8)

    def scatter(send, recv, ssem, rsem):
        here = core * NZ + z

        def step(i, carry):
            d = step_of(i)
            r = (z + d + NZ) % NZ
            for to_core in (core, other):
                remote(send.at[to_core * NZ + r], recv.at[here], ssem, rsem, at(d, 0, to_core)).start()
            return carry

        lax.fori_loop(0, NZ - 1, step, 0)
        remote(send.at[other * NZ + z], recv.at[here], ssem, rsem, at(0, 0, other)).start()
        pltpu.make_async_copy(send.at[core * NZ + z], recv.at[here], rsem).start()

    scatter(kv_send, kv_recv, kv_ss, kv_rs)

    for j in range(CHUNKS):
        for h in range(2):
            q_send[j, h * NZ : (h + 1) * NZ] = permuted(q_ref, (h * CHUNKS + j) * WIDE)
        scatter(q_send.at[j], q_recv.at[j], q_ss.at[j], q_rs.at[j])

    half = CHUNKS * WIDE
    remote(
        g_ref.at[:, pl.ds(pl.multiple_of(other * half, half), half)], g_buf.at[core], g_ss, g_rs, at(0, 0, other)
    ).start()
    pltpu.make_async_copy(g_ref.at[:, pl.ds(pl.multiple_of(core * half, half), half)], g_buf.at[core], g_rs).start()
    remote(seg_src, seg_band.at[4 + core], seg_ss, seg_rs, at(0, 0, other)).start()
    pltpu.make_async_copy(seg_src, seg_band.at[4 + core], seg_rs).start()
    for dc in (1, 2):
        for to_core in (core, other):
            remote(seg_src, seg_band.at[4 - 2 * dc + core], seg_ss, seg_rs, at(0, dc, to_core)).start()

    drain(seg_band, seg_rs)
    for t in range(2):
        seg_q = seg_band[4 + t, 0:1, :].astype(F32)
        for b in range(5):
            seg_k = jnp.broadcast_to(seg_band[t + b, 0:1, :].astype(F32), (D, D)).T
            allowed = seg_k == seg_q
            if b == 4:
                allowed = allowed & (sub <= lane)
            if t + b < 4:
                allowed = allowed & (sub + ((t + b) * D - 2 * ROWS + c * ROWS) >= 0)
            bias[t, b * D : (b + 1) * D, :] = jnp.where(allowed, 0.0, NEG)

    drain(kv_recv, kv_rs)
    band[2 * ROWS :, :] = kv_recv[...].astype(F32).reshape(ROWS, 2 * WIDE).astype(BF16)
    mine = band.at[pl.ds(2 * ROWS, ROWS)]
    for dc in (1, 2):
        remote(mine, band.at[pl.ds((2 - dc) * ROWS, ROWS)], halo_ss, halo_rs, at(0, dc, core)).start()
    drain(g_buf, g_rs)
    drain(band.at[pl.ds(0, 2 * ROWS)], halo_rs)

    def chunk(j, carry):
        drain(q_recv.at[j], q_rs.at[j])
        k_at = pl.ds(pl.multiple_of(j * D, D), D)
        v_at = pl.ds(pl.multiple_of(WIDE + j * D, D), D)
        acc_k[BAND:, :] = jnp.zeros((D, D), F32)
        acc_v[BAND:, :] = jnp.zeros((D, D), F32)
        for t in range(2):
            keys = band[t * D : t * D + BAND, k_at]
            values = band[t * D : t * D + BAND, v_at]
            q_rows = q_recv[j, t * NZ : (t + 1) * NZ].astype(F32).reshape(D, WIDE).astype(BF16)
            g_rows = g_buf[t, :, pl.ds(pl.multiple_of(j * WIDE, WIDE), WIDE)]
            queries = jnp.concatenate([q_rows[:, a * D : (a + 1) * D] for a in range(GROUP)], axis=0)
            grads = jnp.concatenate([g_rows[:, a * D : (a + 1) * D] for a in range(GROUP)], axis=0)
            masked = jnp.concatenate([bias[t]] * GROUP, axis=1)
            score = dot(keys, queries, 1, 1) * (SCALE * LOG2E) + masked
            weight = jnp.exp2(score - jnp.max(score, axis=0, keepdims=True))
            prob = weight * (1.0 / jnp.sum(weight, axis=0, keepdims=True))
            prob_low = prob.astype(BF16)
            grad_prob = dot(values, grads, 1, 1)
            delta = jnp.sum(prob_low.astype(F32) * grad_prob, axis=0, keepdims=True)
            grad_score = (prob * (grad_prob - delta) * SCALE).astype(BF16)
            dk = dot(grad_score, queries, 1, 0)
            dv = dot(prob_low, grads, 1, 0)
            if t == 0:
                acc_k[:BAND, :] = dk
                acc_v[:BAND, :] = dv
            else:
                acc_k[D:, :] += dk
                acc_v[D:, :] += dv
            dq = dot(keys, grad_score, 0, 0)
            for a in range(GROUP):
                dq_stage[j, t, :, a * D : (a + 1) * D] = dq[:, a * D : (a + 1) * D].T.astype(BF16)
        for b in range(2):
            part_send[j, b, :, :D] = acc_k[b * ROWS : (b + 1) * ROWS, :].astype(BF16)
            part_send[j, b, :, D:] = acc_v[b * ROWS : (b + 1) * ROWS, :].astype(BF16)
            remote(part_send.at[j, b], part_recv.at[j, b], part_ss.at[j], part_rs.at[j], at(0, b - 2, core)).start()
        own[j, :, :D] = acc_k[2 * ROWS :, :]
        own[j, :, D:] = acc_v[2 * ROWS :, :]
        remote(dq_stage.at[j, other], dq_recv.at[j], dq_ss.at[j], dq_rs.at[j], at(0, 0, other)).start()
        return carry

    lax.fori_loop(0, CHUNKS, chunk, 0)

    def fold(j, carry):
        drain(part_recv.at[j], part_rs.at[j])
        total = own[j] + part_recv[j, 0].astype(F32) + part_recv[j, 1].astype(F32)
        dkv_send[j] = total.reshape(2, D, 2 * D).astype(BF16)
        remote(dkv_send.at[j, other], dkv_recv.at[j], dkv_ss.at[j], dkv_rs.at[j], at(0, 0, other)).start()
        return carry

    lax.fori_loop(0, CHUNKS, fold, 0)
    for j in range(CHUNKS):
        dq_out[core, :, j * WIDE : (j + 1) * WIDE] = dq_stage[j, core]
        dk_out[core, :, j * D : (j + 1) * D] = dkv_send[j, core, :, :D]
        dv_out[core, :, j * D : (j + 1) * D] = dkv_send[j, core, :, D:]
    for j in range(CHUNKS):
        drain(dq_recv.at[j], dq_rs.at[j])
        dq_out[other, :, j * WIDE : (j + 1) * WIDE] = dq_recv[j]
        drain(dkv_recv.at[j], dkv_rs.at[j])
        dk_out[other, :, j * D : (j + 1) * D] = dkv_recv[j, :, :D]
        dv_out[other, :, j * D : (j + 1) * D] = dkv_recv[j, :, D:]

    drain(kv_send.at[pl.ds(0, 2 * NZ - 1)], kv_ss)
    drain(g_buf.at[0], g_ss)
    drain(seg_band.at[pl.ds(0, 5)], seg_ss)
    drain(band.at[pl.ds(0, 2 * ROWS)], halo_ss)
    for j in range(CHUNKS):
        drain(q_send.at[j, pl.ds(0, 2 * NZ - 1)], q_ss.at[j])
        drain(part_send.at[j], part_ss.at[j])
        drain(dq_recv.at[j], dq_ss.at[j])
        drain(dkv_recv.at[j], dkv_ss.at[j])


def body(query_rows, source_key_rows, source_value_rows, grad_rows, routes, segments):
    dma = pltpu.SemaphoreType.DMA
    vmem = pltpu.VMEM
    call = pl.pallas_call(
        kernel,
        out_shape=(
            jax.ShapeDtypeStruct((2, D, CHUNKS * WIDE), BF16),
            jax.ShapeDtypeStruct((2, D, CHUNKS * D), BF16),
            jax.ShapeDtypeStruct((2, D, CHUNKS * D), BF16),
        ),
        in_specs=[pl.BlockSpec(memory_space=vmem)] * 6,
        out_specs=[pl.BlockSpec(memory_space=vmem)] * 3,
        scratch_shapes=[
            vmem((2 * NZ, CAP, 2 * WIDE), BF16),
            vmem((2 * NZ, CAP, 2 * WIDE), BF16),
            vmem((CHUNKS, 2 * NZ, CAP, WIDE), BF16),
            vmem((CHUNKS, 2 * NZ, CAP, WIDE), BF16),
            vmem((2, D, CHUNKS * WIDE), BF16),
            vmem((3 * ROWS, 2 * WIDE), BF16),
            vmem((8, D), jnp.int32),
            vmem((6, 8, D), jnp.int32),
            vmem((2, BAND, D), F32),
            vmem((3 * ROWS, D), F32),
            vmem((3 * ROWS, D), F32),
            vmem((CHUNKS, ROWS, 2 * D), F32),
            vmem((CHUNKS, 2, ROWS, 2 * D), BF16),
            vmem((CHUNKS, 2, ROWS, 2 * D), BF16),
            vmem((CHUNKS, 2, D, WIDE), BF16),
            vmem((CHUNKS, D, WIDE), BF16),
            vmem((CHUNKS, 2, D, 2 * D), BF16),
            vmem((CHUNKS, D, 2 * D), BF16),
            dma, dma, dma((CHUNKS,)), dma((CHUNKS,)), dma, dma, dma, dma, dma, dma,
            dma((CHUNKS,)), dma((CHUNKS,)), dma((CHUNKS,)), dma((CHUNKS,)), dma((CHUNKS,)), dma((CHUNKS,)),
        ],
        compiler_params=pltpu.CompilerParams(
            collective_id=0, has_side_effects=True, vmem_limit_bytes=56 << 20
        ),
    )
    dq, dk, dv = call(query_rows, source_key_rows, source_value_rows, grad_rows, routes, segments)

    def rows_first(halves):
        return halves.transpose(1, 0, 2).reshape(halves.shape[1], -1)

    return rows_first(dq), rows_first(dk), rows_first(dv)


def solution(mesh):
    placed = (P(("dp", "seq"), None),) * 5 + (P("dp", "seq"),)
    return jax.shard_map(
        body,
        mesh=mesh,
        in_specs=placed,
        out_specs=(P(("dp", "seq"), None),) * 3,
        check_vma=False,
    )
```

```python
import functools

import jax
import jax.numpy as jnp
from jax import lax
from jax.experimental import pallas as pl
from jax.experimental.pallas import tpu as pltpu
from jax.sharding import PartitionSpec as P

MESH = pl.DeviceIdType.MESH
D = 128
GROUP = 4
CHUNKS = 4
NZ = 16
NC = 16
CAP = 8
ROWS = 2 * D
BAND = 5 * D
WIDE = GROUP * D
SCALE = D ** (-0.5)
LOG2E = 1.4426950408889634
NEG = -1e30
F32, BF16 = jnp.float32, jnp.bfloat16


def dot(a, b, ca, cb):
    return lax.dot_general(a, b, (((ca,), (cb,)), ((), ())), preferred_element_type=F32)


def kernel(
    q_hbm, k_hbm, v_hbm, g_hbm, routes_ref, seg_ref,
    dq_out, dk_out, dv_out,
    q_in, kv_in, kv_send, kv_recv, q_send, q_recv, g_buf, band, seg_src, seg_band, bias,
    acc, part_send, part_recv, dq_stage,
    in_s, kv_ss, kv_rs, q_ss, q_rs, g_ss, g_rs, seg_ss, seg_rs, halo_ss, halo_rs,
    part_ss, part_rs, dq_ss, dq_rs,
):
    z = lax.axis_index("dp")
    s = lax.axis_index("seq")
    c, core = s // 2, s % 2
    other = 1 - core
    half = CHUNKS * WIDE

    def at(dz, dc, to_core):
        return {"dp": lax.rem(z + dz + NZ, NZ), "seq": lax.rem(c + dc + NC, NC) * 2 + to_core}

    def remote(src, dst, ssem, rsem, device):
        return pltpu.make_async_remote_copy(
            src_ref=src, dst_ref=dst, send_sem=ssem, recv_sem=rsem,
            device_id=device, device_id_type=MESH,
        )

    def drain(ref, sem):
        pltpu.make_async_copy(ref, ref, sem).wait()

    def columns(start, size):
        return pl.ds(pl.multiple_of(start, size), size)

    def step_of(i):
        return (i // 2 + 1) * (1 - 2 * (i % 2))

    loads = [
        pltpu.make_async_copy(k_hbm, kv_in.at[0], in_s.at[0]),
        pltpu.make_async_copy(v_hbm, kv_in.at[1], in_s.at[1]),
        pltpu.make_async_copy(q_hbm, q_in, in_s.at[2]),
    ]
    for load in loads:
        load.start()

    barrier = pltpu.get_barrier_semaphore()

    def greet(dz, dc, to_core):
        pl.semaphore_signal(barrier, inc=1, device_id=at(dz, dc, to_core), device_id_type=MESH)

    def greet_z(i, carry):
        greet(step_of(i), 0, core)
        greet(step_of(i), 0, other)
        return carry

    lax.fori_loop(0, NZ - 1, greet_z, 0)
    greet(0, 0, other)
    for dc in (1, 2, -1, -2):
        greet(0, dc, core)
        greet(0, dc, other)

    lane = lax.broadcasted_iota(jnp.int32, (D, D), 1)
    sub = lax.broadcasted_iota(jnp.int32, (D, D), 0)
    routes = routes_ref[...]
    onehot = (routes == sub).astype(F32)
    before = dot(onehot.astype(BF16), (sub < lane).astype(BF16), 1, 0)
    rank = jnp.sum(before * onehot, axis=0, keepdims=True)
    slot = routes.astype(F32) * float(CAP) + rank
    order = (slot == sub.astype(F32)).astype(BF16)

    def permuted(rows):
        return dot(order, rows, 1, 0).reshape(NZ, CAP, WIDE).astype(BF16)

    for i in range(2):
        loads[i].wait()
        for h in range(2):
            moved = permuted(kv_in[i, :, h * WIDE : (h + 1) * WIDE])
            for j in range(CHUNKS):
                first = (2 * j + i) * D
                kv_send[h * NZ : (h + 1) * NZ, :, first : first + D] = moved[:, :, j * D : (j + 1) * D]

    pl.semaphore_wait(barrier, 2 * (NZ - 1) + 1 + 8)

    def scatter(send, recv, ssem, rsem):
        here = core * NZ + z

        def step(i, carry):
            d = step_of(NZ - 2 - i)
            r = lax.rem(z + d + NZ, NZ)
            for to_core in (core, other):
                remote(send.at[to_core * NZ + r], recv.at[here], ssem, rsem, at(d, 0, to_core)).start()
            return carry

        lax.fori_loop(0, NZ - 1, step, 0)
        remote(send.at[other * NZ + z], recv.at[here], ssem, rsem, at(0, 0, other)).start()
        pltpu.make_async_copy(send.at[core * NZ + z], recv.at[here], rsem).start()

    scatter(kv_send, kv_recv, kv_ss, kv_rs)

    loads[2].wait()
    for j in range(CHUNKS):
        for h in range(2):
            first = (h * CHUNKS + j) * WIDE
            q_send[j, h * NZ : (h + 1) * NZ] = permuted(q_in[:, first : first + WIDE])

    def send_queries(j, carry):
        scatter(q_send.at[j], q_recv.at[j], q_ss.at[j], q_rs.at[j])
        return carry

    lax.fori_loop(0, 4, send_queries, 0)
    seg_src[...] = jnp.broadcast_to(seg_ref[...], seg_src.shape)
    remote(seg_src, seg_band.at[4 + core], seg_ss, seg_rs, at(0, 0, other)).start()
    pltpu.make_async_copy(seg_src, seg_band.at[4 + core], seg_rs).start()
    for dc in (1, 2):
        for to_core in (core, other):
            remote(seg_src, seg_band.at[4 - 2 * dc + core], seg_ss, seg_rs, at(0, dc, to_core)).start()
    remote(g_hbm.at[:, columns(other * half, half)], g_buf.at[core], g_ss, g_rs, at(0, 0, other)).start()
    pltpu.make_async_copy(g_hbm.at[:, columns(core * half, half)], g_buf.at[core], g_rs).start()

    drain(seg_band, seg_rs)
    for t in range(2):
        seg_q = seg_band[4 + t, 0:1, :].astype(F32)
        for b in range(5):
            seg_k = jnp.broadcast_to(seg_band[t + b, 0:1, :].astype(F32), (D, D)).T
            allowed = seg_k == seg_q
            if b == 4:
                allowed = allowed & (sub <= lane)
            if t + b < 4:
                allowed = allowed & (sub + ((t + b) * D - 2 * ROWS + c * ROWS) >= 0)
            bias[t, b * D : (b + 1) * D, :] = jnp.where(allowed, 0.0, NEG)

    drain(kv_recv, kv_rs)
    for j in range(CHUNKS):
        rows = kv_recv[:, :, 2 * j * D : 2 * (j + 1) * D].astype(F32).reshape(ROWS, 2 * D)
        band[j, 2 * ROWS :, :] = rows.astype(BF16)
        mine = band.at[j, pl.ds(2 * ROWS, ROWS)]
        for dc in (1, 2):
            remote(mine, band.at[j, pl.ds((2 - dc) * ROWS, ROWS)], halo_ss.at[j], halo_rs.at[j], at(0, dc, core)).start()
    drain(g_buf, g_rs)

    def send_part(j, b):
        to = part_recv.at[j, 2 - b // 2, core]
        remote(part_send.at[j, b], to, part_ss.at[j], part_rs.at[j], at(0, b // 2 - 2, b % 2)).start()

    def chunk(j):
        drain(band.at[j, pl.ds(0, 2 * ROWS)], halo_rs.at[j])
        drain(q_recv.at[j], q_rs.at[j])
        for t in range(2):
            keys = band[j, t * D : t * D + BAND, :D]
            values = band[j, t * D : t * D + BAND, D:]
            q_rows = q_recv[j, t * NZ : (t + 1) * NZ].astype(F32).reshape(D, WIDE).astype(BF16)
            g_rows = g_buf[t, :, columns(j * WIDE, WIDE)]
            queries = jnp.concatenate([q_rows[:, a * D : (a + 1) * D] for a in range(GROUP)], axis=0)
            grads = jnp.concatenate([g_rows[:, a * D : (a + 1) * D] for a in range(GROUP)], axis=0)
            masked = jnp.concatenate([bias[t]] * GROUP, axis=1)
            score = dot(keys, queries, 1, 1) * (SCALE * LOG2E) + masked
            weight = jnp.exp2(score - jnp.max(score, axis=0, keepdims=True))
            prob = weight * (1.0 / jnp.sum(weight, axis=0, keepdims=True))
            prob_low = prob.astype(BF16)
            grad_prob = dot(values, grads, 1, 1)
            delta = jnp.sum(prob_low.astype(F32) * grad_prob, axis=0, keepdims=True)
            grad_score = (prob * (grad_prob - delta) * SCALE).astype(BF16)
            dk = dot(grad_score, queries, 1, 0)
            dv = dot(prob_low, grads, 1, 0)
            dq = dot(keys, grad_score, 0, 0)
            for a in range(GROUP):
                dq_stage[j, t, :, a * D : (a + 1) * D] = dq[:, a * D : (a + 1) * D].T.astype(BF16)
            if t == 0:
                acc[:, :D] = dk
                acc[:, D:] = dv
                part_send[j, 0, :, :D] = dk[:D].astype(BF16)
                part_send[j, 0, :, D:] = dv[:D].astype(BF16)
                send_part(j, 0)
            else:
                for b in range(1, 6):
                    rows = slice(b * D, (b + 1) * D)
                    if b < 5:
                        k_sum, v_sum = acc[rows, :D], acc[rows, D:]
                    k_new, v_new = dk[(b - 1) * D : b * D], dv[(b - 1) * D : b * D]
                    k_sum = k_new if b == 5 else k_sum + k_new
                    v_sum = v_new if b == 5 else v_sum + v_new
                    part_send[j, b, :, :D] = k_sum.astype(BF16)
                    part_send[j, b, :, D:] = v_sum.astype(BF16)
        for b in range(1, 4):
            send_part(j, b)
        remote(part_send.at[j, 4 + other], part_recv.at[j, 0, core], part_ss.at[j], part_rs.at[j], at(0, 0, other)).start()
        pltpu.make_async_copy(part_send.at[j, 4 + core], part_recv.at[j, 0, core], part_rs.at[j]).start()
        to = dq_out.at[:, columns(core * half + j * WIDE, WIDE)]
        remote(dq_stage.at[j, other], to, dq_ss.at[j], dq_rs.at[j], at(0, 0, other)).start()
        pltpu.make_async_copy(dq_stage.at[j, core], to, dq_rs.at[j]).start()

    def fold(j):
        drain(part_recv.at[j], part_rs.at[j])
        for h in range(2):
            total = part_recv[j, 0, h].astype(F32) + part_recv[j, 1, h].astype(F32) + part_recv[j, 2, h].astype(F32)
            total = total.astype(BF16)
            dk_out[:, columns(h * WIDE + j * D, D)] = total[:, :D]
            dv_out[:, columns(h * WIDE + j * D, D)] = total[:, D:]

    def turn(j, carry):
        chunk(j)

        @pl.when(j > 0)
        def _():
            fold(j - 1)

        return carry

    lax.fori_loop(0, CHUNKS, turn, 0)
    fold(CHUNKS - 1)

    drain(kv_send.at[pl.ds(0, 2 * NZ - 1)], kv_ss)
    drain(g_buf.at[0], g_ss)
    drain(seg_band.at[pl.ds(0, 5)], seg_ss)
    for j in range(CHUNKS):
        drain(q_send.at[j, pl.ds(0, 2 * NZ - 1)], q_ss.at[j])
        drain(part_send.at[j, pl.ds(0, 5)], part_ss.at[j])
        drain(band.at[j, pl.ds(0, 2 * ROWS)], halo_ss.at[j])
        drain(dq_stage.at[j, 0], dq_ss.at[j])
        drain(dq_stage.at[j], dq_rs.at[j])


def body(query_rows, source_key_rows, source_value_rows, grad_rows, routes, segments):
    dma = pltpu.SemaphoreType.DMA
    vmem = pltpu.VMEM
    here = pl.BlockSpec(memory_space=vmem)
    apart = pl.BlockSpec(memory_space=pl.ANY)
    return pl.pallas_call(
        kernel,
        out_shape=(
            vmem((D, 2 * CHUNKS * WIDE), BF16),
            vmem((D, 2 * CHUNKS * D), BF16),
            vmem((D, 2 * CHUNKS * D), BF16),
        ),
        in_specs=[apart] * 4 + [here] * 2,
        out_specs=[here] * 3,
        scratch_shapes=[
            vmem((D, 2 * CHUNKS * WIDE), BF16),
            vmem((2, D, 2 * WIDE), BF16),
            vmem((2 * NZ, CAP, 2 * WIDE), BF16),
            vmem((2 * NZ, CAP, 2 * WIDE), BF16),
            vmem((CHUNKS, 2 * NZ, CAP, WIDE), BF16),
            vmem((CHUNKS, 2 * NZ, CAP, WIDE), BF16),
            vmem((2, D, CHUNKS * WIDE), BF16),
            vmem((CHUNKS, 3 * ROWS, 2 * D), BF16),
            vmem((8, D), jnp.int32),
            vmem((6, 8, D), jnp.int32),
            vmem((2, BAND, D), F32),
            vmem((BAND, 2 * D), F32),
            vmem((CHUNKS, 6, D, 2 * D), BF16),
            vmem((CHUNKS, 3, 2, D, 2 * D), BF16),
            vmem((CHUNKS, 2, D, WIDE), BF16),
            dma((3,)), dma, dma, dma((CHUNKS,)), dma((CHUNKS,)), dma, dma, dma, dma, dma((CHUNKS,)), dma((CHUNKS,)),
            dma((CHUNKS,)), dma((CHUNKS,)), dma((CHUNKS,)), dma((CHUNKS,)),
        ],
        compiler_params=pltpu.CompilerParams(
            collective_id=0, has_side_effects=True, vmem_limit_bytes=56 << 20
        ),
    )(query_rows, source_key_rows, source_value_rows, grad_rows, routes.reshape(1, D), segments)


def solution(mesh):
    placed = (P(("dp", "seq"), None),) * 5 + (P("dp", "seq"),)
    return jax.shard_map(
        body,
        mesh=mesh,
        in_specs=placed,
        out_specs=(P(("dp", "seq"), None),) * 3,
        check_vma=False,
    )
```

```python
import functools

import jax
import jax.numpy as jnp
from jax import lax
from jax.experimental import pallas as pl
from jax.experimental.pallas import tpu as pltpu
from jax.sharding import PartitionSpec as P

MESH = pl.DeviceIdType.MESH
D = 128
GROUP = 4
CHUNKS = 4
NZ = 16
NC = 16
CAP = 8
ROWS = 2 * D
BAND = 5 * D
WIDE = GROUP * D
SCALE = D ** (-0.5)
LOG2E = 1.4426950408889634
NEG = -1e30
F32, BF16 = jnp.float32, jnp.bfloat16


def dot(a, b, ca, cb):
    return lax.dot_general(a, b, (((ca,), (cb,)), ((), ())), preferred_element_type=F32)


def kernel(
    q_hbm, k_hbm, v_hbm, g_hbm, routes_ref, seg_ref,
    dq_out, dk_out, dv_out,
    q_in, kv_in, kv_send, kv_recv, q_send, q_recv, g_buf, band, seg_src, seg_band, bias,
    part_send, part_recv, dq_stage,
    in_s, kv_ss, kv_rs, q_ss, q_rs, g_ss, g_rs, seg_ss, seg_rs, halo_ss, halo_rs,
    part_ss, part_rs, dq_ss, dq_rs,
):
    z = lax.axis_index("dp")
    s = lax.axis_index("seq")
    c, core = s // 2, s % 2
    other = 1 - core
    half = CHUNKS * WIDE

    def at(dz, dc, to_core):
        return {"dp": lax.rem(z + dz + NZ, NZ), "seq": lax.rem(c + dc + NC, NC) * 2 + to_core}

    def remote(src, dst, ssem, rsem, device):
        return pltpu.make_async_remote_copy(
            src_ref=src, dst_ref=dst, send_sem=ssem, recv_sem=rsem,
            device_id=device, device_id_type=MESH,
        )

    def drain(ref, sem):
        pltpu.make_async_copy(ref, ref, sem).wait()

    def columns(start, size):
        return pl.ds(pl.multiple_of(start, size), size)

    def step_of(i):
        return (i // 2 + 1) * (1 - 2 * (i % 2))

    loads = [
        pltpu.make_async_copy(k_hbm, kv_in.at[0], in_s.at[0]),
        pltpu.make_async_copy(v_hbm, kv_in.at[1], in_s.at[1]),
        pltpu.make_async_copy(q_hbm, q_in, in_s.at[2]),
    ]
    for load in loads:
        load.start()

    barrier = pltpu.get_barrier_semaphore()

    def greet(dz, dc, to_core):
        pl.semaphore_signal(barrier, inc=1, device_id=at(dz, dc, to_core), device_id_type=MESH)

    def greet_z(i, carry):
        greet(step_of(i), 0, core)
        greet(step_of(i), 0, other)
        return carry

    lax.fori_loop(0, NZ - 1, greet_z, 0)
    greet(0, 0, other)
    for dc in (1, 2, -1, -2):
        greet(0, dc, core)
        greet(0, dc, other)

    lane = lax.broadcasted_iota(jnp.int32, (D, D), 1)
    sub = lax.broadcasted_iota(jnp.int32, (D, D), 0)
    routes = routes_ref[...]
    onehot = (routes == sub).astype(F32)
    before = dot(onehot.astype(BF16), (sub < lane).astype(BF16), 1, 0)
    rank = jnp.sum(before * onehot, axis=0, keepdims=True)
    slot = routes.astype(F32) * float(CAP) + rank
    order = (slot == sub.astype(F32)).astype(BF16)

    def permuted(rows):
        return dot(order, rows, 1, 0).reshape(NZ, CAP, WIDE).astype(BF16)

    for i in range(2):
        loads[i].wait()
        for h in range(2):
            moved = permuted(kv_in[i, :, h * WIDE : (h + 1) * WIDE])
            for j in range(CHUNKS):
                first = (2 * j + i) * D
                kv_send[h * NZ : (h + 1) * NZ, :, first : first + D] = moved[:, :, j * D : (j + 1) * D]

    pl.semaphore_wait(barrier, 2 * (NZ - 1) + 1 + 8)

    def scatter(pieces, to_cores):
        here = core * NZ + z

        def step(i, carry):
            d = step_of(NZ - 2 - i)
            r = lax.rem(z + d + NZ, NZ)
            for to_core in to_cores:
                for send, recv, ssem, rsem in pieces:
                    remote(send.at[to_core * NZ + r], recv.at[here], ssem, rsem, at(d, 0, to_core)).start()
            return carry

        lax.fori_loop(0, NZ - 1, step, 0)

    def within(send, recv, ssem, rsem):
        here = core * NZ + z
        remote(send.at[other * NZ + z], recv.at[here], ssem, rsem, at(0, 0, other)).start()
        pltpu.make_async_copy(send.at[core * NZ + z], recv.at[here], rsem).start()

    scatter([(kv_send, kv_recv, kv_ss, kv_rs)], (core, other))
    within(kv_send, kv_recv, kv_ss, kv_rs)

    loads[2].wait()
    for j in range(CHUNKS):
        for h in range(2):
            first = (h * CHUNKS + j) * WIDE
            moved = permuted(q_in[:, first : first + WIDE])
            for w in range(2):
                q_send[j, w, h * NZ : (h + 1) * NZ] = moved[:, :, w * 2 * D : (w + 1) * 2 * D]

    def send_queries(j, carry):
        halves = [(q_send.at[j, w], q_recv.at[j, w], q_ss.at[j, w], q_rs.at[j, w]) for w in range(2)]
        for piece in halves:
            within(*piece)
        for to_core in range(2):
            for piece in halves:
                scatter([piece], (to_core,))
        return carry

    lax.fori_loop(0, 4, send_queries, 0)
    seg_src[...] = jnp.broadcast_to(seg_ref[...], seg_src.shape)
    remote(seg_src, seg_band.at[4 + core], seg_ss, seg_rs, at(0, 0, other)).start()
    pltpu.make_async_copy(seg_src, seg_band.at[4 + core], seg_rs).start()
    for dc in (1, 2):
        for to_core in (core, other):
            remote(seg_src, seg_band.at[4 - 2 * dc + core], seg_ss, seg_rs, at(0, dc, to_core)).start()
    remote(g_hbm.at[:, columns(other * half, half)], g_buf.at[core], g_ss, g_rs, at(0, 0, other)).start()
    pltpu.make_async_copy(g_hbm.at[:, columns(core * half, half)], g_buf.at[core], g_rs).start()

    drain(seg_band, seg_rs)
    for t in range(2):
        seg_q = seg_band[4 + t, 0:1, :].astype(F32)
        for b in range(5):
            seg_k = jnp.broadcast_to(seg_band[t + b, 0:1, :].astype(F32), (D, D)).T
            allowed = seg_k == seg_q
            if b == 4:
                allowed = allowed & (sub <= lane)
            if t + b < 4:
                allowed = allowed & (sub + ((t + b) * D - 2 * ROWS + c * ROWS) >= 0)
            bias[t, b * D : (b + 1) * D, :] = jnp.where(allowed, 0.0, NEG)

    drain(kv_recv, kv_rs)
    for j in range(CHUNKS):
        rows = kv_recv[:, :, 2 * j * D : 2 * (j + 1) * D].astype(F32).reshape(ROWS, 2 * D)
        band[j, 2 * ROWS :, :] = rows.astype(BF16)
        mine = band.at[j, pl.ds(2 * ROWS, ROWS)]
        for dc in (1, 2):
            remote(mine, band.at[j, pl.ds((2 - dc) * ROWS, ROWS)], halo_ss.at[j], halo_rs.at[j], at(0, dc, core)).start()
    drain(g_buf, g_rs)

    def spread(j, i, first, second):
        def send(b, device):
            to = part_recv.at[j, i, 2 - b // 2, core]
            remote(part_send.at[j, i, b], to, part_ss.at[j], part_rs.at[j], device).start()

        for b in range(6):
            total = first[b * D : (b + 1) * D] if b < 5 else second[4 * D :]
            if 0 < b < 5:
                total = total + second[(b - 1) * D : b * D]
            part_send[j, i, b] = total.astype(BF16)
            if b < 4:
                send(b, at(0, b // 2 - 2, b % 2))
        send(4 + other, at(0, 0, other))
        pltpu.make_async_copy(part_send.at[j, i, 4 + core], part_recv.at[j, i, 0, core], part_rs.at[j]).start()

    def chunk(j):
        drain(band.at[j, pl.ds(0, 2 * ROWS)], halo_rs.at[j])
        keys = [band[j, t * D : t * D + BAND, :D] for t in range(2)]
        values = [band[j, t * D : t * D + BAND, D:] for t in range(2)]
        sums = {}
        for w in range(2):
            drain(q_recv.at[j, w], q_rs.at[j, w])
            queries, grads, probs, lows, scores = ([] for _ in range(5))
            for t in range(2):
                q_rows = q_recv[j, w, t * NZ : (t + 1) * NZ].astype(F32).reshape(D, 2 * D).astype(BF16)
                g_rows = g_buf[t, :, columns(j * WIDE + w * 2 * D, 2 * D)]
                queries.append(jnp.concatenate([q_rows[:, :D], q_rows[:, D:]], axis=0))
                grads.append(jnp.concatenate([g_rows[:, :D], g_rows[:, D:]], axis=0))
                masked = jnp.concatenate([bias[t]] * 2, axis=1)
                score = dot(keys[t], queries[t], 1, 1) * (SCALE * LOG2E) + masked
                weight = jnp.exp2(score - jnp.max(score, axis=0, keepdims=True))
                probs.append(weight * (1.0 / jnp.sum(weight, axis=0, keepdims=True)))
                lows.append(probs[t].astype(BF16))
                dv = dot(lows[t], grads[t], 1, 0)
                sums[1, t] = dv if w == 0 else sums[1, t] + dv
            if w == 1:
                spread(j, 1, sums[1, 0], sums[1, 1])
            for t in range(2):
                grad_prob = dot(values[t], grads[t], 1, 1)
                delta = jnp.sum(lows[t].astype(F32) * grad_prob, axis=0, keepdims=True)
                scores.append((probs[t] * (grad_prob - delta) * SCALE).astype(BF16))
                dk = dot(scores[t], queries[t], 1, 0)
                sums[0, t] = dk if w == 0 else sums[0, t] + dk
            if w == 1:
                spread(j, 0, sums[0, 0], sums[0, 1])
            for t in range(2):
                dq = dot(keys[t], scores[t], 0, 0)
                for a in range(2):
                    first = (2 * w + a) * D
                    dq_stage[j, t, :, first : first + D] = dq[:, a * D : (a + 1) * D].T.astype(BF16)
        to = dq_out.at[:, columns(core * half + j * WIDE, WIDE)]
        remote(dq_stage.at[j, other], to, dq_ss.at[j], dq_rs.at[j], at(0, 0, other)).start()
        pltpu.make_async_copy(dq_stage.at[j, core], to, dq_rs.at[j]).start()

    def fold(j):
        drain(part_recv.at[j], part_rs.at[j])
        for i, out in enumerate((dk_out, dv_out)):
            for h in range(2):
                near, mid, far = (part_recv[j, i, n, h].astype(F32) for n in range(3))
                out[:, columns(h * WIDE + j * D, D)] = (near + mid + far).astype(BF16)

    def turn(j, carry):
        chunk(j)

        @pl.when(j > 0)
        def _():
            fold(j - 1)

        return carry

    lax.fori_loop(0, CHUNKS, turn, 0)
    fold(CHUNKS - 1)

    drain(kv_send.at[pl.ds(0, 2 * NZ - 1)], kv_ss)
    drain(g_buf.at[0], g_ss)
    drain(seg_band.at[pl.ds(0, 5)], seg_ss)
    for j in range(CHUNKS):
        for w in range(2):
            drain(q_send.at[j, w, pl.ds(0, 2 * NZ - 1)], q_ss.at[j, w])
        drain(part_send.at[j, :, pl.ds(0, 5)], part_ss.at[j])
        drain(band.at[j, pl.ds(0, 2 * ROWS)], halo_ss.at[j])
        drain(dq_stage.at[j, 0], dq_ss.at[j])
        drain(dq_stage.at[j], dq_rs.at[j])


def body(query_rows, source_key_rows, source_value_rows, grad_rows, routes, segments):
    dma = pltpu.SemaphoreType.DMA
    vmem = pltpu.VMEM
    here = pl.BlockSpec(memory_space=vmem)
    apart = pl.BlockSpec(memory_space=pl.ANY)
    outs = pl.pallas_call(
        kernel,
        out_shape=(
            vmem((D, 2 * CHUNKS * WIDE), BF16),
            vmem((D, 2 * CHUNKS * D), BF16),
            vmem((D, 2 * CHUNKS * D), BF16),
        ),
        in_specs=[apart] * 4 + [here] * 2,
        out_specs=[here] * 3,
        scratch_shapes=[
            vmem((D, 2 * CHUNKS * WIDE), BF16),
            vmem((2, D, 2 * WIDE), BF16),
            vmem((2 * NZ, CAP, 2 * WIDE), BF16),
            vmem((2 * NZ, CAP, 2 * WIDE), BF16),
            vmem((CHUNKS, 2, 2 * NZ, CAP, 2 * D), BF16),
            vmem((CHUNKS, 2, 2 * NZ, CAP, 2 * D), BF16),
            vmem((2, D, CHUNKS * WIDE), BF16),
            vmem((CHUNKS, 3 * ROWS, 2 * D), BF16),
            vmem((8, D), jnp.int32),
            vmem((6, 8, D), jnp.int32),
            vmem((2, BAND, D), F32),
            vmem((CHUNKS, 2, 6, D, D), BF16),
            vmem((CHUNKS, 2, 3, 2, D, D), BF16),
            vmem((CHUNKS, 2, D, WIDE), BF16),
            dma((3,)), dma, dma, dma((CHUNKS, 2)), dma((CHUNKS, 2)), dma, dma, dma, dma, dma((CHUNKS,)), dma((CHUNKS,)),
            dma((CHUNKS,)), dma((CHUNKS,)), dma((CHUNKS,)), dma((CHUNKS,)),
        ],
        compiler_params=pltpu.CompilerParams(
            collective_id=0, has_side_effects=True, vmem_limit_bytes=56 << 20
        ),
    )(query_rows, source_key_rows, source_value_rows, grad_rows, routes.reshape(1, D), segments)
    outs = [pltpu.with_memory_space_constraint(out, vmem) for out in outs]
    return pl.pallas_call(
        finish,
        out_shape=tuple(jax.ShapeDtypeStruct(o.shape, o.dtype) for o in outs),
        in_specs=[here] * 3,
        out_specs=[apart] * 3,
        scratch_shapes=[dma((3,))],
    )(*outs)


def finish(*refs):
    sems = refs[-1]
    copies = [pltpu.make_async_copy(refs[i], refs[3 + i], sems.at[i]) for i in range(3)]
    for copy in copies:
        copy.start()
    for copy in copies:
        copy.wait()


def solution(mesh):
    placed = (P(("dp", "seq"), None),) * 5 + (P("dp", "seq"),)
    return jax.shard_map(
        body,
        mesh=mesh,
        in_specs=placed,
        out_specs=(P(("dp", "seq"), None),) * 3,
        check_vma=False,
    )
```

```python
import functools

import jax
import jax.numpy as jnp
from jax import lax
from jax.experimental import pallas as pl
from jax.experimental.pallas import tpu as pltpu
from jax.sharding import PartitionSpec as P

MESH = pl.DeviceIdType.MESH
D = 128
GROUP = 4
CHUNKS = 4
NZ = 16
NC = 16
CAP = 8
ROWS = 2 * D
BAND = 5 * D
WIDE = GROUP * D
SCALE = D ** (-0.5)
LOG2E = 1.4426950408889634
NEG = -1e30
F32, BF16 = jnp.float32, jnp.bfloat16


def dot(a, b, ca, cb):
    return lax.dot_general(a, b, (((ca,), (cb,)), ((), ())), preferred_element_type=F32)


def kernel(
    q_hbm, k_hbm, v_hbm, g_hbm, routes_ref, seg_ref,
    dq_out, dk_out, dv_out,
    q_in, kv_in, kv_send, kv_recv, q_send, q_recv, g_buf, band, seg_src, seg_band, bias,
    part_send, part_recv, dq_stage,
    in_s, kv_ss, kv_rs, q_ss, q_rs, g_ss, g_rs, seg_ss, seg_rs, halo_ss, halo_rs,
    part_ss, part_rs, dq_ss, dq_rs,
):
    z = lax.axis_index("dp")
    s = lax.axis_index("seq")
    c, core = s // 2, s % 2
    other = 1 - core
    half = CHUNKS * WIDE

    def at(dz, dc, to_core):
        return {"dp": lax.rem(z + dz + NZ, NZ), "seq": lax.rem(c + dc + NC, NC) * 2 + to_core}

    def remote(src, dst, ssem, rsem, device):
        return pltpu.make_async_remote_copy(
            src_ref=src, dst_ref=dst, send_sem=ssem, recv_sem=rsem,
            device_id=device, device_id_type=MESH,
        )

    def drain(ref, sem):
        pltpu.make_async_copy(ref, ref, sem).wait()

    def columns(start, size):
        return pl.ds(pl.multiple_of(start, size), size)

    def step_of(i):
        return (i // 2 + 1) * (1 - 2 * (i % 2))

    loads = [
        pltpu.make_async_copy(k_hbm, kv_in.at[0], in_s.at[0]),
        pltpu.make_async_copy(v_hbm, kv_in.at[1], in_s.at[1]),
        pltpu.make_async_copy(q_hbm, q_in, in_s.at[2]),
    ]
    for load in loads:
        load.start()

    barrier = pltpu.get_barrier_semaphore()

    def greet(dz, dc, to_core):
        pl.semaphore_signal(barrier, inc=1, device_id=at(dz, dc, to_core), device_id_type=MESH)

    def greet_z(i, carry):
        greet(step_of(i), 0, core)
        greet(step_of(i), 0, other)
        return carry

    lax.fori_loop(0, NZ - 1, greet_z, 0)
    greet(0, 0, other)
    for dc in (1, 2, -1, -2):
        greet(0, dc, core)
        greet(0, dc, other)

    lane = lax.broadcasted_iota(jnp.int32, (D, D), 1)
    sub = lax.broadcasted_iota(jnp.int32, (D, D), 0)
    routes = routes_ref[...]
    onehot = (routes == sub).astype(F32)
    before = dot(onehot.astype(BF16), (sub < lane).astype(BF16), 1, 0)
    rank = jnp.sum(before * onehot, axis=0, keepdims=True)
    slot = routes.astype(F32) * float(CAP) + rank
    order = (slot == sub.astype(F32)).astype(BF16)

    def permuted(rows):
        return dot(order, rows, 1, 0).reshape(NZ, CAP, WIDE).astype(BF16)

    for i in range(2):
        loads[i].wait()
        for h in range(2):
            moved = permuted(kv_in[i, :, h * WIDE : (h + 1) * WIDE])
            for j in range(CHUNKS):
                first = (2 * j + i) * D
                kv_send[h * NZ : (h + 1) * NZ, :, first : first + D] = moved[:, :, j * D : (j + 1) * D]

    pl.semaphore_wait(barrier, 2 * (NZ - 1) + 1 + 8)

    def scatter(pieces, to_cores):
        here = core * NZ + z

        def step(i, carry):
            d = step_of(NZ - 2 - i)
            r = lax.rem(z + d + NZ, NZ)
            for to_core in to_cores:
                for send, recv, ssem, rsem in pieces:
                    remote(send.at[to_core * NZ + r], recv.at[here], ssem, rsem, at(d, 0, to_core)).start()
            return carry

        lax.fori_loop(0, NZ - 1, step, 0)

    def within(send, recv, ssem, rsem):
        here = core * NZ + z
        remote(send.at[other * NZ + z], recv.at[here], ssem, rsem, at(0, 0, other)).start()
        pltpu.make_async_copy(send.at[core * NZ + z], recv.at[here], rsem).start()

    scatter([(kv_send, kv_recv, kv_ss, kv_rs)], (core, other))
    within(kv_send, kv_recv, kv_ss, kv_rs)

    loads[2].wait()
    for j in range(CHUNKS):
        for h in range(2):
            first = (h * CHUNKS + j) * WIDE
            moved = permuted(q_in[:, first : first + WIDE])
            for w in range(2):
                q_send[j, w, h * NZ : (h + 1) * NZ] = moved[:, :, w * 2 * D : (w + 1) * 2 * D]

    def send_queries(j, carry):
        halves = [(q_send.at[j, w], q_recv.at[j, w], q_ss.at[j, w], q_rs.at[j, w]) for w in range(2)]
        for piece in halves:
            within(*piece)
        for to_core in range(2):
            for piece in halves:
                scatter([piece], (to_core,))
        return carry

    lax.fori_loop(0, 4, send_queries, 0)
    seg_src[...] = jnp.broadcast_to(seg_ref[...], seg_src.shape)
    remote(seg_src, seg_band.at[4 + core], seg_ss, seg_rs, at(0, 0, other)).start()
    pltpu.make_async_copy(seg_src, seg_band.at[4 + core], seg_rs).start()
    for dc in (1, 2):
        for to_core in (core, other):
            remote(seg_src, seg_band.at[4 - 2 * dc + core], seg_ss, seg_rs, at(0, dc, to_core)).start()
    remote(g_hbm.at[:, columns(other * half, half)], g_buf.at[core], g_ss, g_rs, at(0, 0, other)).start()
    pltpu.make_async_copy(g_hbm.at[:, columns(core * half, half)], g_buf.at[core], g_rs).start()

    drain(seg_band, seg_rs)
    for t in range(2):
        seg_q = seg_band[4 + t, 0:1, :].astype(F32)
        for b in range(5):
            seg_k = jnp.broadcast_to(seg_band[t + b, 0:1, :].astype(F32), (D, D)).T
            allowed = seg_k == seg_q
            if b == 4:
                allowed = allowed & (sub <= lane)
            if t + b < 4:
                allowed = allowed & (sub + ((t + b) * D - 2 * ROWS + c * ROWS) >= 0)
            bias[t, b * D : (b + 1) * D, :] = jnp.where(allowed, 0.0, NEG)

    drain(kv_recv, kv_rs)
    for j in range(CHUNKS):
        rows = kv_recv[:, :, 2 * j * D : 2 * (j + 1) * D].astype(F32).reshape(ROWS, 2 * D)
        band[j, 2 * ROWS :, :] = rows.astype(BF16)
        mine = band.at[j, pl.ds(2 * ROWS, ROWS)]
        for dc in (1, 2):
            remote(mine, band.at[j, pl.ds((2 - dc) * ROWS, ROWS)], halo_ss.at[j], halo_rs.at[j], at(0, dc, core)).start()
    drain(g_buf, g_rs)

    def spread(j, i, first, second):
        def send(b, device):
            to = part_recv.at[j, i, 2 - b // 2, core]
            remote(part_send.at[j, i, b], to, part_ss.at[j], part_rs.at[j, i], device).start()

        for b in range(6):
            total = first[b * D : (b + 1) * D] if b < 5 else second[4 * D :]
            if 0 < b < 5:
                total = total + second[(b - 1) * D : b * D]
            part_send[j, i, b] = total.astype(BF16)
            if b < 4:
                send(b, at(0, b // 2 - 2, b % 2))
        send(4 + other, at(0, 0, other))
        pltpu.make_async_copy(part_send.at[j, i, 4 + core], part_recv.at[j, i, 0, core], part_rs.at[j, i]).start()

    def chunk(j):
        drain(band.at[j, pl.ds(0, 2 * ROWS)], halo_rs.at[j])
        keys = [band[j, t * D : t * D + BAND, :D] for t in range(2)]
        values = [band[j, t * D : t * D + BAND, D:] for t in range(2)]
        sums = {}
        for w in range(2):
            drain(q_recv.at[j, w], q_rs.at[j, w])
            queries, grads, probs, lows, scores = ([] for _ in range(5))
            for t in range(2):
                q_rows = q_recv[j, w, t * NZ : (t + 1) * NZ].astype(F32).reshape(D, 2 * D).astype(BF16)
                g_rows = g_buf[t, :, columns(j * WIDE + w * 2 * D, 2 * D)]
                queries.append(jnp.concatenate([q_rows[:, :D], q_rows[:, D:]], axis=0))
                grads.append(jnp.concatenate([g_rows[:, :D], g_rows[:, D:]], axis=0))
                masked = jnp.concatenate([bias[t]] * 2, axis=1)
                score = dot(keys[t], queries[t], 1, 1) * (SCALE * LOG2E) + masked
                weight = jnp.exp2(score - jnp.max(score, axis=0, keepdims=True))
                probs.append(weight * (1.0 / jnp.sum(weight, axis=0, keepdims=True)))
                lows.append(probs[t].astype(BF16))
                dv = dot(lows[t], grads[t], 1, 0)
                sums[1, t] = dv if w == 0 else sums[1, t] + dv
            if w == 1:
                spread(j, 1, sums[1, 0], sums[1, 1])
            for t in range(2):
                grad_prob = dot(values[t], grads[t], 1, 1)
                delta = jnp.sum(lows[t].astype(F32) * grad_prob, axis=0, keepdims=True)
                scores.append((probs[t] * (grad_prob - delta) * SCALE).astype(BF16))
                dk = dot(scores[t], queries[t], 1, 0)
                sums[0, t] = dk if w == 0 else sums[0, t] + dk
            if w == 1:
                spread(j, 0, sums[0, 0], sums[0, 1])
            for t in range(2):
                dq = dot(keys[t], scores[t], 0, 0)
                for a in range(2):
                    dq_stage[j, w, t, :, a * D : (a + 1) * D] = dq[:, a * D : (a + 1) * D].T.astype(BF16)
            to = dq_out.at[:, columns(core * half + (2 * j + w) * 2 * D, 2 * D)]
            remote(dq_stage.at[j, w, other], to, dq_ss.at[j, w], dq_rs.at[j, w], at(0, 0, other)).start()
            pltpu.make_async_copy(dq_stage.at[j, w, core], to, dq_rs.at[j, w]).start()

    def fold(j):
        for i, out in ((1, dv_out), (0, dk_out)):
            drain(part_recv.at[j, i], part_rs.at[j, i])
            for h in range(2):
                near, mid, far = (part_recv[j, i, n, h].astype(F32) for n in range(3))
                out[:, columns(h * WIDE + j * D, D)] = (near + mid + far).astype(BF16)

    def turn(j, carry):
        chunk(j)

        @pl.when(j > 0)
        def _():
            fold(j - 1)

        return carry

    lax.fori_loop(0, CHUNKS, turn, 0)
    fold(CHUNKS - 1)

    drain(kv_send.at[pl.ds(0, 2 * NZ - 1)], kv_ss)
    drain(g_buf.at[0], g_ss)
    drain(seg_band.at[pl.ds(0, 5)], seg_ss)
    for j in range(CHUNKS):
        for w in range(2):
            drain(q_send.at[j, w, pl.ds(0, 2 * NZ - 1)], q_ss.at[j, w])
        drain(part_send.at[j, :, pl.ds(0, 5)], part_ss.at[j])
        drain(band.at[j, pl.ds(0, 2 * ROWS)], halo_ss.at[j])
        for w in range(2):
            drain(dq_stage.at[j, w, 0], dq_ss.at[j, w])
            drain(dq_stage.at[j, w], dq_rs.at[j, w])


def body(query_rows, source_key_rows, source_value_rows, grad_rows, routes, segments):
    dma = pltpu.SemaphoreType.DMA
    vmem = pltpu.VMEM
    here = pl.BlockSpec(memory_space=vmem)
    apart = pl.BlockSpec(memory_space=pl.ANY)
    outs = pl.pallas_call(
        kernel,
        out_shape=(
            vmem((D, 2 * CHUNKS * WIDE), BF16),
            vmem((D, 2 * CHUNKS * D), BF16),
            vmem((D, 2 * CHUNKS * D), BF16),
        ),
        in_specs=[apart] * 4 + [here] * 2,
        out_specs=[here] * 3,
        scratch_shapes=[
            vmem((D, 2 * CHUNKS * WIDE), BF16),
            vmem((2, D, 2 * WIDE), BF16),
            vmem((2 * NZ, CAP, 2 * WIDE), BF16),
            vmem((2 * NZ, CAP, 2 * WIDE), BF16),
            vmem((CHUNKS, 2, 2 * NZ, CAP, 2 * D), BF16),
            vmem((CHUNKS, 2, 2 * NZ, CAP, 2 * D), BF16),
            vmem((2, D, CHUNKS * WIDE), BF16),
            vmem((CHUNKS, 3 * ROWS, 2 * D), BF16),
            vmem((8, D), jnp.int32),
            vmem((6, 8, D), jnp.int32),
            vmem((2, BAND, D), F32),
            vmem((CHUNKS, 2, 6, D, D), BF16),
            vmem((CHUNKS, 2, 3, 2, D, D), BF16),
            vmem((CHUNKS, 2, 2, D, 2 * D), BF16),
            dma((3,)), dma, dma, dma((CHUNKS, 2)), dma((CHUNKS, 2)), dma, dma, dma, dma, dma((CHUNKS,)), dma((CHUNKS,)),
            dma((CHUNKS,)), dma((CHUNKS, 2)), dma((CHUNKS, 2)), dma((CHUNKS, 2)),
        ],
        compiler_params=pltpu.CompilerParams(
            collective_id=0, has_side_effects=True, vmem_limit_bytes=56 << 20
        ),
    )(query_rows, source_key_rows, source_value_rows, grad_rows, routes.reshape(1, D), segments)
    outs = [pltpu.with_memory_space_constraint(out, vmem) for out in outs]
    return pl.pallas_call(
        finish,
        out_shape=tuple(jax.ShapeDtypeStruct(o.shape, o.dtype) for o in outs),
        in_specs=[here] * 3,
        out_specs=[apart] * 3,
        scratch_shapes=[dma((3,))],
    )(*outs)


def finish(*refs):
    sems = refs[-1]
    copies = [pltpu.make_async_copy(refs[i], refs[3 + i], sems.at[i]) for i in range(3)]
    for copy in copies:
        copy.start()
    for copy in copies:
        copy.wait()


def solution(mesh):
    placed = (P(("dp", "seq"), None),) * 5 + (P("dp", "seq"),)
    return jax.shard_map(
        body,
        mesh=mesh,
        in_specs=placed,
        out_specs=(P(("dp", "seq"), None),) * 3,
        check_vma=False,
    )
```
